32 devices in a mesh: expert: 4 (over y, x), inner: 8 (over z, core).
Axes of the slice: x: 2, y: 2, z: 4, core: 2. Of those that a mesh axis runs over, the one named last changes fastest.
Arguments:
- tokens: bfloat16 [512, 3072], P('expert', 'inner'), may hold values from -6 to 6
- cotangent: bfloat16 [512, 3072], P('expert', 'inner'), may hold values from -6 to 6
- routes: int32 [512, 2], P('expert'), may hold values from 0 to 3, all different within a row; in each aligned block of 128 rows (0 to 127, 128 to 255, ...) at most 80 rows name the same one
- probs: float32 [512, 2], P('expert'), may hold values from 0.1 to 1
- w_gate: bfloat16 [4, 3072, 8192], P('expert', 'inner'), may hold values from -0.109375 to 0.109375
- w_up: bfloat16 [4, 3072, 8192], P('expert', 'inner'), may hold values from -0.109375 to 0.109375
- w_down: bfloat16 [4, 3072, 8192], P('expert', 'inner'), may hold values from -0.09375 to 0.09375
Outputs:
- layer_out: bfloat16 [512, 3072], P('expert', 'inner')
- grad_gate: bfloat16 [4, 3072, 8192], P('expert', None, 'inner')
- grad_up: bfloat16 [4, 3072, 8192], P('expert', None, 'inner')
- grad_down: bfloat16 [4, 3072, 8192], P('expert', None, 'inner')
The draws below stay inside these ranges and needn't reach their ends.
Inputs may be any that keep to these rules, and one draw needn't show every extreme that they name: `routes`: each token names two different experts; within each block of 128 tokens no expert is named by more than 80 tokens, and in every draw some expert is named by exactly 80 tokens of some block.
All inputs are finite; a program needn't handle non-finite values.
Results may differ from the reference program's by a relative error of at most 0.0057.
Values may be sent and summed in bfloat16 or wider, within the bound.
A program may use at most 128 MiB of HBM per device.

```python
import math
import jax
import jax.numpy as jnp
import numpy as np
from jax import lax

D = 3072
FF = 8192
TOP = 2
TOK_GRP = 128
EXPERTS = 4
C = 80
TOKENS = 512
N_EXPERT = 4


def with_spikes(result, rng, source, target, blocks, factor):
    def block_of(position):
        return (jnp.arange(result.shape[position]) // (result.shape[position] // blocks)).reshape((-1,) + (1,) * (result.ndim - 1 - position))

    one_side = jax.random.permutation(rng, blocks)[block_of(target)]
    second = (block_of(target) + blocks // 2) % blocks
    return jnp.where((block_of(source) == one_side) | (block_of(source) == second), factor * result, result)


def level_of(rng, extent, split, least, top_value):
    def one(dim, parts):
        heights = jax.random.uniform(jax.random.fold_in(jax.random.fold_in(rng, 6), dim), (parts,), jnp.float32, least / len(split), top_value / len(split))
        return jnp.repeat(jnp.exp(heights), extent[dim] // parts).reshape((-1,) + (1,) * (len(extent) - dim - 1))

    loudness = one(*split[0])
    for cut in split[1:]:
        loudness = loudness * one(*cut)
    return loudness


def routed_block(stream_key, own, number, rows, number_of, top, limit, skew):
    order = jax.random.permutation(stream_key, number_of)
    heavy_load, ordinary = portions_of(number_of, rows * top, limit, skew, True), portions_of(number_of, rows * top, limit, skew, False)
    places = jnp.arange(number_of)

    def named(tallies, offset_by):
        used = int((tallies > 0).sum())
        fixed = max(1, used // 4)
        shifted = fixed + (places - fixed + offset_by * (used - fixed)) % max(1, number_of - fixed)
        return jnp.zeros((number_of,), jnp.int32).at[order[jnp.where(places < fixed, places, shifted)]].set(jnp.asarray(tallies, jnp.int32))

    tallies = jnp.where(number % 4 == 0, named(heavy_load, number // 4), named(ordinary, number - number // 4 - 1))
    mixed = jax.random.permutation(jax.random.fold_in(own, 3), number_of)
    giver, receiver = mixed[0:number_of // 2 * 2:2], mixed[1:number_of // 2 * 2:2]
    margin = jnp.minimum(tallies[giver] - 1, limit - tallies[receiver]) // 2
    margin = jnp.where((giver == order[0]) | (receiver == order[0]) | (tallies[receiver] == 0), 0, jnp.maximum(margin, 0))
    shifted = jax.random.randint(jax.random.fold_in(own, 4), (number_of // 2,), 0, 1 << 20) % (margin + 1)
    tallies = tallies.at[giver].add(-shifted).at[receiver].add(shifted)
    labels = jnp.searchsorted(jnp.cumsum(tallies), jnp.arange(rows * top), side="right").astype(jnp.int32)
    table = labels.reshape(top, rows).T
    table = table[jax.random.permutation(jax.random.fold_in(own, 1), rows)]
    offset_by = jax.random.randint(jax.random.fold_in(own, 2), (rows, 1), 0, top)
    return jnp.take_along_axis(table, (jnp.arange(top)[None, :] + offset_by) % top, axis=1)


def portions_of(amount, total, limit, slope, full):
    weights = [(1 << 20) // math.isqrt(standing ** slope) + 1 for standing in range(1, amount + 1)]
    largest = limit if full else min(limit, max(-(-total // amount), total * weights[0] // sum(weights)))
    least = 1 if total - largest >= amount - 1 else 0
    given, rest = [largest] + [least] * (amount - 1), total - largest - least * (amount - 1)
    while rest > 0:
        candidates = [i for i in range(1, amount) if given[i] < largest] or [i for i in range(1, amount) if given[i] < limit]
        pool, left = sum([weights[i] for i in candidates]), rest
        for i in candidates:
            more = min(limit - given[i], max(1, left * weights[i] // pool), rest)
            given[i] = given[i] + more
            rest = rest - more
    return np.array(given)


def centred(rng, extent, spread, reach, cuts=(), kind=jnp.bfloat16):
    entries = jax.random.normal(rng, extent, jnp.float32) * spread
    if len(cuts) > 0:
        entries = level_of(rng, extent, cuts, -0.22, 0.18) * entries
    return jnp.clip(entries, min=-reach, max=reach).astype(kind)


def gaussian_with(key, dims, deviation, reach, pieces, heavy, kind=jnp.bfloat16):
    drawn = deviation * jax.random.normal(key, dims, jnp.float32)
    if pieces:
        drawn = drawn * level_of(key, dims, pieces, -0.22, 0.18)
    return jnp.clip(with_spikes(drawn, jax.random.fold_in(key, 3), *heavy), -reach, reach).astype(kind)


def setup_inputs(seed: int = 0) -> dict:
    key_of = jax.random.split(jax.random.key(seed), 8)
    tokens = centred(key_of[0], (TOKENS, D), 1.0, 6.0, ((0, 4), (1, 8)))
    cotangent = centred(key_of[1], (TOKENS, D), 1.0, 6.0, ((0, 4), (1, 8)))
    routes_keys = jax.random.split(jax.random.fold_in(key_of[2], 1), TOKENS // TOK_GRP)
    routes_turns = jax.random.permutation(jax.random.fold_in(key_of[2], 3), TOKENS // TOK_GRP)
    routes = jax.vmap(lambda own, number: routed_block(jax.random.fold_in(key_of[2], 2), own, number, TOK_GRP, EXPERTS, 2, C, 1))(routes_keys, routes_turns).reshape((TOKENS, TOP))
    probs = jnp.clip(0.1 + 0.9 * jax.random.uniform(key_of[3], (TOKENS, TOP), jnp.float32) ** level_of(key_of[3], (TOKENS, TOP), ((0, 4),), -0.2, 0.2), 0.1, 1.0)
    w_gate = centred(key_of[4], (EXPERTS, D, FF), D ** -0.5, 0.109375, ((0, 4), (1, 8)))
    w_up = centred(key_of[5], (EXPERTS, D, FF), D ** -0.5, 0.109375, ((0, 4), (1, 8)))
    w_down = gaussian_with(key_of[6], (EXPERTS, D, FF), FF ** -0.5, 0.09375, ((0, 4), (1, 8)), (2, 1, 8, 2.0))
    return {"tokens": tokens, "cotangent": cotangent, "routes": routes, "probs": probs, "w_gate": w_gate, "w_up": w_up, "w_down": w_down}


def expert_pass(operands):
    rows_x, rows_g, gate_w, up_w, down_w = operands
    gate_pre = jnp.dot(rows_x, gate_w, preferred_element_type=jnp.float32)
    up_pre = jnp.dot(rows_x, up_w, preferred_element_type=jnp.float32)
    sigmoid_gate = jax.nn.sigmoid(gate_pre)
    activated = gate_pre * sigmoid_gate
    hidden = (activated * up_pre).astype(jnp.bfloat16)
    expert_out = jnp.dot(hidden, down_w.T, preferred_element_type=jnp.float32).astype(jnp.bfloat16)
    hidden_grad = jnp.dot(rows_g, down_w, preferred_element_type=jnp.float32)
    up_grad = (hidden_grad * activated).astype(jnp.bfloat16)
    gate_grad = (hidden_grad * up_pre * sigmoid_gate * (1.0 + gate_pre * (1.0 - sigmoid_gate))).astype(jnp.bfloat16)
    grad_down = jnp.dot(rows_g.T, hidden, preferred_element_type=jnp.float32).astype(jnp.bfloat16)
    grad_gate = jnp.dot(rows_x.T, gate_grad, preferred_element_type=jnp.float32).astype(jnp.bfloat16)
    grad_up = jnp.dot(rows_x.T, up_grad, preferred_element_type=jnp.float32).astype(jnp.bfloat16)
    return expert_out, grad_gate, grad_up, grad_down


def reference(tokens, cotangent, routes, probs, w_gate, w_up, w_down):
    group_count = N_EXPERT
    capacity = C
    routed = routes.reshape(group_count, TOK_GRP * 2)
    expert_ids = jnp.arange(EXPERTS, dtype=jnp.int32)
    onehot = (routed[:, :, None] == expert_ids[None, None, :]).astype(jnp.int32)
    rank_in = (jnp.cumsum(onehot, axis=1) - 1).astype(jnp.int32)
    slot_of = jnp.sum(rank_in * onehot, axis=2).astype(jnp.int32)
    group_ids = jnp.arange(group_count, dtype=jnp.int32)[:, None]
    target = (routed * (group_count * capacity) + group_ids * capacity + slot_of).reshape(-1).astype(jnp.int32)
    pair_x = jnp.repeat(tokens, 2, axis=0)
    scaled = (probs.reshape(-1, 1) * jnp.repeat(cotangent, 2, axis=0).astype(jnp.float32)).astype(jnp.bfloat16)
    slot_total = EXPERTS * group_count * capacity
    buffer_x = jnp.zeros((slot_total, D), jnp.bfloat16).at[target].set(pair_x)
    buffer_g = jnp.zeros((slot_total, D), jnp.bfloat16).at[target].set(scaled)
    results = lax.map(expert_pass, (buffer_x.reshape(EXPERTS, -1, D), buffer_g.reshape(EXPERTS, -1, D), w_gate, w_up, w_down))
    expert_out = results[0].reshape(slot_total, D)
    picked = expert_out[target].astype(jnp.float32).reshape(TOKENS, 2, D)
    layer_out = (probs[:, 0:1] * picked[:, 0, :] + probs[:, 1:2] * picked[:, 1, :]).astype(jnp.bfloat16)
    return layer_out, results[1], results[2], results[3]
```

```python
import jax
import jax.numpy as jnp
from jax import lax
from jax.sharding import PartitionSpec as P


def place_rows(picks, values):
    return lax.dot_general(
        picks, values, (((0,), (0,)), ((), ())), preferred_element_type=jnp.float32
    )


def per_device_exchange(tokens, cotangent, routes, probs, w_gate, w_up, w_down):
    group_count = lax.axis_size("expert")
    tok_count = tokens.shape[0]
    capacity = min(tok_count, 5 * tok_count // (2 * group_count))
    slot_total = group_count * capacity
    gate_cols, up_cols, down_cols = (
        lax.all_to_all(w_gate, "inner", split_axis=2, concat_axis=1, tiled=True),
        lax.all_to_all(w_up, "inner", split_axis=2, concat_axis=1, tiled=True),
        lax.all_to_all(w_down, "inner", split_axis=2, concat_axis=1, tiled=True),
    )
    expert_ids = jnp.arange(group_count, dtype=jnp.int32)
    onehot = (routes[:, :, None] == expert_ids[None, None, :]).astype(jnp.int32)
    flat_hits = onehot.reshape(tok_count * 2, group_count)
    rank_in = jnp.cumsum(flat_hits, axis=0) - 1
    slot_of = jnp.sum(rank_in * flat_hits, axis=1).reshape(tok_count, 2)
    target = routes * capacity + slot_of
    positions = jnp.arange(slot_total, dtype=jnp.int32)
    pick_first = (target[:, 0:1] == positions[None, :]).astype(jnp.bfloat16)
    pick_second = (target[:, 1:2] == positions[None, :]).astype(jnp.bfloat16)
    feat_x, feat_g = (tokens, cotangent)
    row_width = feat_x.shape[1]
    grads_float = feat_g.astype(jnp.float32)
    scaled_first = (probs[:, 0:1] * grads_float).astype(jnp.bfloat16)
    scaled_second = (probs[:, 1:2] * grads_float).astype(jnp.bfloat16)
    send_x = place_rows(pick_first + pick_second, feat_x).astype(jnp.bfloat16)
    send_g = (place_rows(pick_first, scaled_first) + place_rows(pick_second, scaled_second)).astype(
        jnp.bfloat16
    )
    recv_x, recv_g = (
        lax.all_to_all(
            send_x.reshape(group_count, capacity, row_width),
            "expert",
            split_axis=0,
            concat_axis=0,
            tiled=True,
        ),
        lax.all_to_all(
            send_g.reshape(group_count, capacity, row_width),
            "expert",
            split_axis=0,
            concat_axis=0,
            tiled=True,
        ),
    )
    rows_x, rows_g = (
        lax.all_gather(recv_x, "inner", axis=2, tiled=True),
        lax.all_gather(recv_g, "inner", axis=2, tiled=True),
    )
    rows_x = rows_x.reshape(slot_total, -1)
    rows_g = rows_g.reshape(slot_total, -1)
    gate_w = gate_cols[0]
    up_w = up_cols[0]
    down_w = down_cols[0]
    gate_pre = jnp.dot(rows_x, gate_w, preferred_element_type=jnp.float32)
    up_pre = jnp.dot(rows_x, up_w, preferred_element_type=jnp.float32)
    sigmoid_gate = jax.nn.sigmoid(gate_pre)
    activated = gate_pre * sigmoid_gate
    hidden = (activated * up_pre).astype(jnp.bfloat16)
    partial_value = lax.dot_general(
        hidden, down_w, (((1,), (1,)), ((), ())), preferred_element_type=jnp.float32
    )
    expert_out = lax.psum_scatter(partial_value, "inner", scatter_dimension=1, tiled=True).astype(
        jnp.bfloat16
    )
    returned = lax.all_to_all(
        expert_out.reshape(group_count, capacity, -1),
        "expert",
        split_axis=0,
        concat_axis=0,
        tiled=True,
    ).reshape(slot_total, -1)
    first_out = jnp.dot(pick_first, returned, preferred_element_type=jnp.float32)
    second_out = jnp.dot(pick_second, returned, preferred_element_type=jnp.float32)
    layer_out = (probs[:, 0:1] * first_out + probs[:, 1:2] * second_out).astype(jnp.bfloat16)
    hidden_grad = jnp.dot(rows_g, down_w, preferred_element_type=jnp.float32)
    up_grad = (hidden_grad * activated).astype(jnp.bfloat16)
    gate_grad = (
        hidden_grad * up_pre * sigmoid_gate * (1.0 + gate_pre * (1.0 - sigmoid_gate))
    ).astype(jnp.bfloat16)
    grad_down = place_rows(rows_g, hidden).astype(jnp.bfloat16)[None]
    grad_gate = place_rows(rows_x, gate_grad).astype(jnp.bfloat16)[None]
    grad_up = place_rows(rows_x, up_grad).astype(jnp.bfloat16)[None]
    return (layer_out, grad_gate, grad_up, grad_down)


def shifted(chips, sources, step):
    return [(2 * s + k, 2 * (s + step) + k) for s in sources for k in (0, 1)]


def per_device_line(tokens, cotangent, routes, probs, w_gate, w_up, w_down):
    group_count = lax.axis_size("expert")
    inner = lax.axis_size("inner")
    chips = inner // 2
    last = chips - 1
    me = lax.axis_index("inner")
    chip, core = me // 2, me % 2
    tok_count, feat = tokens.shape
    width = w_gate.shape[2] // inner
    capacity = min(tok_count, 5 * tok_count // (2 * group_count))
    slot_total = group_count * capacity
    partner = [(i, i ^ 1) for i in range(inner)]

    def columns(w, chunk, which):
        return lax.dynamic_slice(w, (0, (2 * chunk + which) * width), (feat, width))

    def from_partner(w):
        theirs = jnp.concatenate([columns(w, q, 1 - core) for q in range(chips)], axis=1)
        return lax.ppermute(theirs, "inner", partner)

    gate_w, up_w, down_w = w_gate[0], w_up[0], w_down[0]
    gate_o, up_o, down_o = from_partner(gate_w), from_partner(up_w), from_partner(down_w)

    expert_ids = jnp.arange(group_count, dtype=jnp.int32)
    onehot = (routes[:, :, None] == expert_ids[None, None, :]).astype(jnp.int32)
    flat_hits = onehot.reshape(tok_count * 2, group_count)
    rank_in = jnp.cumsum(flat_hits, axis=0) - 1
    slot_of = jnp.sum(rank_in * flat_hits, axis=1).reshape(tok_count, 2)
    target = routes * capacity + slot_of
    positions = jnp.arange(slot_total, dtype=jnp.int32)
    pick_first = (target[:, 0:1] == positions[None, :]).astype(jnp.bfloat16)
    pick_second = (target[:, 1:2] == positions[None, :]).astype(jnp.bfloat16)
    grads_float = cotangent.astype(jnp.float32)
    scaled_first = (probs[:, 0:1] * grads_float).astype(jnp.bfloat16)
    scaled_second = (probs[:, 1:2] * grads_float).astype(jnp.bfloat16)
    send_x = place_rows(pick_first + pick_second, tokens).astype(jnp.bfloat16)
    send_g = (place_rows(pick_first, scaled_first) + place_rows(pick_second, scaled_second)).astype(
        jnp.bfloat16
    )
    both = jnp.concatenate([send_x, send_g], axis=1).reshape(group_count, capacity, 2 * feat)
    rows = lax.all_to_all(both, "expert", split_axis=0, concat_axis=0, tiled=True)
    rows = rows.reshape(slot_total, 2 * feat)
    rows_o = lax.ppermute(rows, "inner", partner)

    def partial_of(first, w, other_w):
        mine, theirs = rows[:, first : first + feat], rows_o[:, first : first + feat]

        def part(chunk):
            chunk = jnp.clip(chunk, 0, last)
            return jnp.dot(
                mine, columns(w, chunk, core), preferred_element_type=jnp.float32
            ) + jnp.dot(
                theirs,
                lax.dynamic_slice(other_w, (0, chunk * width), (feat, width)),
                preferred_element_type=jnp.float32,
            )

        return part

    def add_in(value, *arrived):
        for one in arrived:
            if one is not None:
                value = value + one.astype(jnp.float32)
        return value

    def reduce_line(part):
        in_r = in_l = None
        for t in range(last):
            to_r, to_l = last + chip - t, chip + t - last
            if 2 * t < last:
                out_r = out_l = add_in(
                    part(jnp.where(chip <= t, to_r, to_l)), in_r, in_l
                ).astype(jnp.bfloat16)
            else:
                out_r = add_in(part(to_r), in_r).astype(jnp.bfloat16)
                out_l = add_in(part(to_l), in_l).astype(jnp.bfloat16)
            perm_r = shifted(chips, range(0, t + 1), 1)
            perm_l = shifted(chips, range(last - t, chips), -1)
            if 2 * t < last - 2:
                in_r, in_l = lax.ppermute(out_r, "inner", perm_r + perm_l), None
            else:
                in_r = lax.ppermute(out_r, "inner", perm_r)
                in_l = lax.ppermute(out_l, "inner", perm_l)
        return add_in(part(chip), in_r, in_l)

    def gather_line(value):
        found = []
        from_l = from_r = value
        for s in range(last):
            from_l = lax.ppermute(from_l, "inner", shifted(chips, range(s, last), 1))
            from_r = lax.ppermute(from_r, "inner", shifted(chips, range(1, chips - s), -1))
            found.append((from_l, from_r))
        return found

    gate_pre = reduce_line(partial_of(0, gate_w, gate_o))
    up_pre = reduce_line(partial_of(0, up_w, up_o))
    sigmoid_gate = jax.nn.sigmoid(gate_pre)
    activated = gate_pre * sigmoid_gate
    hidden = (activated * up_pre).astype(jnp.bfloat16)
    pieces = gather_line(hidden)
    hidden_grad = reduce_line(partial_of(feat, down_w, down_o))
    row_pieces = gather_line(rows)

    def out_of(piece, chunk):
        chunk = jnp.clip(chunk, 0, last)
        dims = (((1,), (1,)), ((), ()))
        kept = lax.dot_general(
            piece, columns(down_w, chunk, core), dims, preferred_element_type=jnp.float32
        )
        sent = lax.dot_general(
            piece,
            lax.dynamic_slice(down_o, (0, chunk * width), (feat, width)),
            dims,
            preferred_element_type=jnp.float32,
        )
        return kept, sent

    kept, sent = out_of(hidden, chip)
    for s, (from_l, from_r) in enumerate(pieces):
        near_l, near_r = chip - 1 - s, chip + 1 + s
        if 2 * s <= last - 2:
            terms = [(from_l, near_l), (from_r, near_r)]
        else:
            terms = [(jnp.where(near_l >= 0, from_l, from_r), jnp.where(near_l >= 0, near_l, near_r))]
        for piece, chunk in terms:
            more_kept, more_sent = out_of(piece, chunk)
            kept, sent = kept + more_kept, sent + more_sent
    expert_out = (kept + lax.ppermute(sent, "inner", partner)).astype(jnp.bfloat16)
    returned = lax.all_to_all(
        expert_out.reshape(group_count, capacity, -1),
        "expert",
        split_axis=0,
        concat_axis=0,
        tiled=True,
    ).reshape(slot_total, -1)
    first_out = jnp.dot(pick_first, returned, preferred_element_type=jnp.float32)
    second_out = jnp.dot(pick_second, returned, preferred_element_type=jnp.float32)
    layer_out = (probs[:, 0:1] * first_out + probs[:, 1:2] * second_out).astype(jnp.bfloat16)

    ordered = []
    for q in range(chips):
        pick = rows
        for s, (from_l, from_r) in enumerate(row_pieces):
            pick = jnp.where(chip - 1 - s == q, from_l, jnp.where(chip + 1 + s == q, from_r, pick))
        ordered.append(pick)
    mine = jnp.stack(ordered)
    theirs = lax.ppermute(mine, "inner", partner)
    even, odd = jnp.where(core == 0, mine, theirs), jnp.where(core == 0, theirs, mine)

    def all_rows(first):
        parts = []
        for q in range(chips):
            parts += [even[q][:, first : first + feat], odd[q][:, first : first + feat]]
        return jnp.concatenate(parts, axis=1)

    rows_x, rows_g = all_rows(0), all_rows(feat)
    up_grad = (hidden_grad * activated).astype(jnp.bfloat16)
    gate_grad = (
        hidden_grad * up_pre * sigmoid_gate * (1.0 + gate_pre * (1.0 - sigmoid_gate))
    ).astype(jnp.bfloat16)
    grad_down = place_rows(rows_g, hidden).astype(jnp.bfloat16)[None]
    grad_gate = place_rows(rows_x, gate_grad).astype(jnp.bfloat16)[None]
    grad_up = place_rows(rows_x, up_grad).astype(jnp.bfloat16)[None]
    return (layer_out, grad_gate, grad_up, grad_down)


def solution(mesh):
    placed = (
        P("expert", "inner"),
        P("expert", "inner"),
        P("expert", None),
        P("expert", None),
        P("expert", "inner", None),
        P("expert", "inner", None),
        P("expert", "inner", None),
    )
    short = mesh.shape["inner"] <= 16
    return jax.shard_map(
        per_device_line if short else per_device_exchange,
        mesh=mesh,
        in_specs=placed,
        out_specs=(
            P("expert", "inner"),
            P("expert", None, "inner"),
            P("expert", None, "inner"),
            P("expert", None, "inner"),
        ),
        check_vma=False,
    )
```

```python
import jax
import jax.numpy as jnp
from jax import lax
from jax.sharding import PartitionSpec as P


def place_rows(picks, values):
    return lax.dot_general(
        picks, values, (((0,), (0,)), ((), ())), preferred_element_type=jnp.float32
    )


def per_device_exchange(tokens, cotangent, routes, probs, w_gate, w_up, w_down):
    group_count = lax.axis_size("expert")
    tok_count = tokens.shape[0]
    capacity = min(tok_count, 5 * tok_count // (2 * group_count))
    slot_total = group_count * capacity
    gate_cols, up_cols, down_cols = (
        lax.all_to_all(w_gate, "inner", split_axis=2, concat_axis=1, tiled=True),
        lax.all_to_all(w_up, "inner", split_axis=2, concat_axis=1, tiled=True),
        lax.all_to_all(w_down, "inner", split_axis=2, concat_axis=1, tiled=True),
    )
    expert_ids = jnp.arange(group_count, dtype=jnp.int32)
    onehot = (routes[:, :, None] == expert_ids[None, None, :]).astype(jnp.int32)
    flat_hits = onehot.reshape(tok_count * 2, group_count)
    rank_in = jnp.cumsum(flat_hits, axis=0) - 1
    slot_of = jnp.sum(rank_in * flat_hits, axis=1).reshape(tok_count, 2)
    target = routes * capacity + slot_of
    positions = jnp.arange(slot_total, dtype=jnp.int32)
    pick_first = (target[:, 0:1] == positions[None, :]).astype(jnp.bfloat16)
    pick_second = (target[:, 1:2] == positions[None, :]).astype(jnp.bfloat16)
    feat_x, feat_g = (tokens, cotangent)
    row_width = feat_x.shape[1]
    grads_float = feat_g.astype(jnp.float32)
    scaled_first = (probs[:, 0:1] * grads_float).astype(jnp.bfloat16)
    scaled_second = (probs[:, 1:2] * grads_float).astype(jnp.bfloat16)
    send_x = place_rows(pick_first + pick_second, feat_x).astype(jnp.bfloat16)
    send_g = (place_rows(pick_first, scaled_first) + place_rows(pick_second, scaled_second)).astype(
        jnp.bfloat16
    )
    recv_x, recv_g = (
        lax.all_to_all(
            send_x.reshape(group_count, capacity, row_width),
            "expert",
            split_axis=0,
            concat_axis=0,
            tiled=True,
        ),
        lax.all_to_all(
            send_g.reshape(group_count, capacity, row_width),
            "expert",
            split_axis=0,
            concat_axis=0,
            tiled=True,
        ),
    )
    rows_x, rows_g = (
        lax.all_gather(recv_x, "inner", axis=2, tiled=True),
        lax.all_gather(recv_g, "inner", axis=2, tiled=True),
    )
    rows_x = rows_x.reshape(slot_total, -1)
    rows_g = rows_g.reshape(slot_total, -1)
    gate_w = gate_cols[0]
    up_w = up_cols[0]
    down_w = down_cols[0]
    gate_pre = jnp.dot(rows_x, gate_w, preferred_element_type=jnp.float32)
    up_pre = jnp.dot(rows_x, up_w, preferred_element_type=jnp.float32)
    sigmoid_gate = jax.nn.sigmoid(gate_pre)
    activated = gate_pre * sigmoid_gate
    hidden = (activated * up_pre).astype(jnp.bfloat16)
    partial_value = lax.dot_general(
        hidden, down_w, (((1,), (1,)), ((), ())), preferred_element_type=jnp.float32
    )
    expert_out = lax.psum_scatter(partial_value, "inner", scatter_dimension=1, tiled=True).astype(
        jnp.bfloat16
    )
    returned = lax.all_to_all(
        expert_out.reshape(group_count, capacity, -1),
        "expert",
        split_axis=0,
        concat_axis=0,
        tiled=True,
    ).reshape(slot_total, -1)
    first_out = jnp.dot(pick_first, returned, preferred_element_type=jnp.float32)
    second_out = jnp.dot(pick_second, returned, preferred_element_type=jnp.float32)
    layer_out = (probs[:, 0:1] * first_out + probs[:, 1:2] * second_out).astype(jnp.bfloat16)
    hidden_grad = jnp.dot(rows_g, down_w, preferred_element_type=jnp.float32)
    up_grad = (hidden_grad * activated).astype(jnp.bfloat16)
    gate_grad = (
        hidden_grad * up_pre * sigmoid_gate * (1.0 + gate_pre * (1.0 - sigmoid_gate))
    ).astype(jnp.bfloat16)
    grad_down = place_rows(rows_g, hidden).astype(jnp.bfloat16)[None]
    grad_gate = place_rows(rows_x, gate_grad).astype(jnp.bfloat16)[None]
    grad_up = place_rows(rows_x, up_grad).astype(jnp.bfloat16)[None]
    return (layer_out, grad_gate, grad_up, grad_down)


def shifted(sources, step):
    return [(2 * s + k, 2 * (s + step) + k) for s in sources for k in (0, 1)]


def per_device_line(tokens, cotangent, routes, probs, w_gate, w_up, w_down):
    group_count = lax.axis_size("expert")
    inner = lax.axis_size("inner")
    chips = inner // 2
    last = chips - 1
    me = lax.axis_index("inner")
    chip, core = me // 2, me % 2
    tok_count, feat = tokens.shape
    width = w_gate.shape[2] // inner
    capacity = min(tok_count, 5 * tok_count // (2 * group_count))
    slot_total = group_count * capacity
    partner = [(i, i ^ 1) for i in range(inner)]

    def send(value, perm):
        return lax.ppermute(value, "inner", perm)

    def columns(w, chunk, which):
        return lax.dynamic_slice(w, (0, (2 * chunk + which) * width), (feat, width))

    def from_partner(w):
        theirs = jnp.concatenate([columns(w, q, 1 - core) for q in range(chips)], axis=1)
        return send(theirs, partner)

    gate_w, up_w, down_w = w_gate[0], w_up[0], w_down[0]
    gate_o, up_o, down_o = (from_partner(gate_w), from_partner(up_w), from_partner(down_w))

    expert_ids = jnp.arange(group_count, dtype=jnp.int32)
    onehot = (routes[:, :, None] == expert_ids[None, None, :]).astype(jnp.int32)
    flat_hits = onehot.reshape(tok_count * 2, group_count)
    rank_in = jnp.cumsum(flat_hits, axis=0) - 1
    slot_of = jnp.sum(rank_in * flat_hits, axis=1).reshape(tok_count, 2)
    target = routes * capacity + slot_of
    positions = jnp.arange(slot_total, dtype=jnp.int32)
    pick_first = (target[:, 0:1] == positions[None, :]).astype(jnp.bfloat16)
    pick_second = (target[:, 1:2] == positions[None, :]).astype(jnp.bfloat16)
    grads_float = cotangent.astype(jnp.float32)
    scaled_first = (probs[:, 0:1] * grads_float).astype(jnp.bfloat16)
    scaled_second = (probs[:, 1:2] * grads_float).astype(jnp.bfloat16)
    send_x = place_rows(pick_first + pick_second, tokens).astype(jnp.bfloat16)
    send_g = (place_rows(pick_first, scaled_first) + place_rows(pick_second, scaled_second)).astype(
        jnp.bfloat16
    )
    both = jnp.concatenate([send_x, send_g], axis=1).reshape(group_count, capacity, 2 * feat)
    rows = lax.all_to_all(both, "expert", split_axis=0, concat_axis=0, tiled=True)
    rows = rows.reshape(slot_total, 2 * feat)
    rows_o = send(rows, partner)

    def partial_of(first, w, other_w):
        mine, theirs = rows[:, first : first + feat], rows_o[:, first : first + feat]

        def part(chunk):
            chunk = jnp.clip(chunk, 0, last)
            return jnp.dot(
                mine, columns(w, chunk, core), preferred_element_type=jnp.float32
            ) + jnp.dot(
                theirs,
                lax.dynamic_slice(other_w, (0, chunk * width), (feat, width)),
                preferred_element_type=jnp.float32,
            )

        return part

    def add_in(value, *arrived):
        for one in arrived:
            if one is not None:
                value = value + one.astype(jnp.float32)
        return value

    def reduce_line(part):
        in_r = in_l = None
        for t in range(last):
            to_r, to_l = last + chip - t, chip + t - last
            if 2 * t < last:
                out_r = out_l = add_in(
                    part(jnp.where(chip <= t, to_r, to_l)), in_r, in_l
                ).astype(jnp.bfloat16)
            else:
                out_r = add_in(part(to_r), in_r).astype(jnp.bfloat16)
                out_l = add_in(part(to_l), in_l).astype(jnp.bfloat16)
            perm_r = shifted(range(0, t + 1), 1)
            perm_l = shifted(range(last - t, chips), -1)
            if 2 * t < last - 2:
                in_r, in_l = send(out_r, perm_r + perm_l), None
            else:
                in_r = send(out_r, perm_r)
                in_l = send(out_l, perm_l)
        return add_in(part(chip), in_r, in_l)

    def gather_line(value):
        found = []
        from_l = from_r = value
        for s in range(last):
            from_l = send(from_l, shifted(range(s, last), 1))
            from_r = send(from_r, shifted(range(1, chips - s), -1))
            found.append((from_l, from_r))
        return found

    gate_pre = reduce_line(partial_of(0, gate_w, gate_o))
    up_pre = reduce_line(partial_of(0, up_w, up_o))
    sigmoid_gate = jax.nn.sigmoid(gate_pre)
    activated = gate_pre * sigmoid_gate
    hidden = (activated * up_pre).astype(jnp.bfloat16)
    pieces = gather_line(hidden)
    hidden_grad = reduce_line(partial_of(feat, down_w, down_o))
    row_pieces = gather_line(rows)

    def out_of(piece, chunk):
        chunk = jnp.clip(chunk, 0, last)
        dims = (((1,), (1,)), ((), ()))
        kept = lax.dot_general(
            piece, columns(down_w, chunk, core), dims, preferred_element_type=jnp.float32
        )
        sent = lax.dot_general(
            piece,
            lax.dynamic_slice(down_o, (0, chunk * width), (feat, width)),
            dims,
            preferred_element_type=jnp.float32,
        )
        return kept, sent

    kept, sent = out_of(hidden, chip)
    for s, (from_l, from_r) in enumerate(pieces):
        near_l, near_r = chip - 1 - s, chip + 1 + s
        if 2 * s <= last - 2:
            terms = [(from_l, near_l), (from_r, near_r)]
        else:
            terms = [(jnp.where(near_l >= 0, from_l, from_r), jnp.where(near_l >= 0, near_l, near_r))]
        for piece, chunk in terms:
            more_kept, more_sent = out_of(piece, chunk)
            kept, sent = kept + more_kept, sent + more_sent
    expert_out = (kept + send(sent, partner)).astype(jnp.bfloat16)
    returned = lax.all_to_all(
        expert_out.reshape(group_count, capacity, -1),
        "expert",
        split_axis=0,
        concat_axis=0,
        tiled=True,
    ).reshape(slot_total, -1)
    first_out = jnp.dot(pick_first, returned, preferred_element_type=jnp.float32)
    second_out = jnp.dot(pick_second, returned, preferred_element_type=jnp.float32)
    layer_out = (probs[:, 0:1] * first_out + probs[:, 1:2] * second_out).astype(jnp.bfloat16)

    ordered = []
    for q in range(chips):
        pick = rows
        for s, (from_l, from_r) in enumerate(row_pieces):
            pick = jnp.where(chip - 1 - s == q, from_l, jnp.where(chip + 1 + s == q, from_r, pick))
        ordered.append(pick)
    mine = jnp.stack(ordered)
    theirs = send(mine, partner)
    even, odd = jnp.where(core == 0, mine, theirs), jnp.where(core == 0, theirs, mine)

    def all_rows(first):
        parts = []
        for q in range(chips):
            parts += [even[q][:, first : first + feat], odd[q][:, first : first + feat]]
        return jnp.concatenate(parts, axis=1)

    rows_x, rows_g = all_rows(0), all_rows(feat)
    up_grad = (hidden_grad * activated).astype(jnp.bfloat16)
    gate_grad = (
        hidden_grad * up_pre * sigmoid_gate * (1.0 + gate_pre * (1.0 - sigmoid_gate))
    ).astype(jnp.bfloat16)
    grad_down = place_rows(rows_g, hidden).astype(jnp.bfloat16)[None]
    grad_gate = place_rows(rows_x, gate_grad).astype(jnp.bfloat16)[None]
    grad_up = place_rows(rows_x, up_grad).astype(jnp.bfloat16)[None]
    return (layer_out, grad_gate, grad_up, grad_down)


def layer(*arrays):
    return per_device_line(*arrays)


def solution(mesh):
    placed = (
        P("expert", "inner"),
        P("expert", "inner"),
        P("expert", None),
        P("expert", None),
        P("expert", "inner", None),
        P("expert", "inner", None),
        P("expert", "inner", None),
    )
    short = mesh.shape["inner"] <= 16
    return jax.shard_map(
        layer if short else per_device_exchange,
        mesh=mesh,
        in_specs=placed,
        out_specs=(
            P("expert", "inner"),
            P("expert", None, "inner"),
            P("expert", None, "inner"),
            P("expert", None, "inner"),
        ),
        check_vma=False,
    )
```
